32 devices in a mesh: dp: 16 (over z, y, core), tensor: 2 (over x).
Axes of the slice: x: 2, y: 2, z: 4, core: 2. Of those that a mesh axis runs over, the one named last changes fastest.
Arguments:
- tokens: float32 [11264, 2048], P(('dp', 'tensor')), may hold values from -6 to 6
- cotangent: float32 [11264, 2048], P(('dp', 'tensor')), may hold values from -6 to 6
- lengths: int32 [16, 13], P('dp'), may hold values from 1 to 176, 704 in all within a row
- parents: int32 [16, 13], P('dp'), may hold values from 0 to 11, as said below
- query_proj: float32 [2048, 2048], P('dp', 'tensor'), may hold values from -0.125 to 0.125
- key_proj: float32 [2048, 2048], P('dp', 'tensor'), may hold values from -0.125 to 0.125
- value_proj: float32 [2048, 2048], P('dp', 'tensor'), may hold values from -0.125 to 0.125
- out_proj: float32 [2048, 2048], P('tensor', 'dp'), may hold values from -0.375 to 0.375
- up_proj: float32 [2048, 8192], P('dp', 'tensor'), may hold values from -0.125 to 0.125
- down_proj: float32 [8192, 2048], P('tensor', 'dp'), may hold values from -0.0625 to 0.0625
- first_gain: float32 [2048], P(('dp', 'tensor')), may hold values from 0.5 to 1.5
- first_shift: float32 [2048], P(('dp', 'tensor')), may hold values from -3 to 3
- query_bias: float32 [2048], P(('dp', 'tensor')), may hold values from -3 to 3
- value_bias: float32 [2048], P(('dp', 'tensor')), may hold values from -3 to 3
- out_bias: float32 [2048], P(('dp', 'tensor')), may hold values from -3 to 3
- second_gain: float32 [2048], P(('dp', 'tensor')), may hold values from 0.5 to 1.5
- second_shift: float32 [2048], P(('dp', 'tensor')), may hold values from -3 to 3
- up_bias: float32 [8192], P(('dp', 'tensor')), may hold values from -3 to 3
- down_bias: float32 [2048], P(('dp', 'tensor')), may hold values from -3 to 3
Outputs:
- layer_output: float32 [11264, 2048], P(('dp', 'tensor'))
- tokens_grad: float32 [11264, 2048], P(('dp', 'tensor'))
- query_proj_grad: float32 [2048, 2048], P('dp', 'tensor')
- key_proj_grad: float32 [2048, 2048], P('dp', 'tensor')
- value_proj_grad: float32 [2048, 2048], P('dp', 'tensor')
- out_proj_grad: float32 [2048, 2048], P('tensor', 'dp')
- up_proj_grad: float32 [2048, 8192], P('dp', 'tensor')
- down_proj_grad: float32 [8192, 2048], P('tensor', 'dp')
- first_gain_grad: float32 [2048], P(('dp', 'tensor'))
- first_shift_grad: float32 [2048], P(('dp', 'tensor'))
- query_bias_grad: float32 [2048], P(('dp', 'tensor'))
- value_bias_grad: float32 [2048], P(('dp', 'tensor'))
- out_bias_grad: float32 [2048], P(('dp', 'tensor'))
- second_gain_grad: float32 [2048], P(('dp', 'tensor'))
- second_shift_grad: float32 [2048], P(('dp', 'tensor'))
- up_bias_grad: float32 [8192], P(('dp', 'tensor'))
- down_bias_grad: float32 [2048], P(('dp', 'tensor'))
The draws below stay inside these ranges and needn't reach their ends.
Inputs may be any that keep to these rules, and one draw needn't show every extreme that they name: parents[t, 0] is 0 and parents[t, s] < s for s >= 1, so every segment follows its parent, and segment 0 is each tree's root; the last segment's parent is segment 13 - 2 in every tree. `lengths`: each row sums to 704, and its largest entry is exactly 176.
All inputs are finite; a program needn't handle non-finite values.
Results may differ from the reference program's by a relative error of at most 0.013.
Values may be sent and summed in bfloat16 or wider, within the bound.
No kernel may reach another device: no remote copies, remote signals or barrier semaphores. Data moves between devices by JAX's collectives and lax.ppermute only.
A program may use at most 384 MiB of HBM per device.

```python
import math
import jax
import jax.numpy as jnp
import numpy as np
from jax import lax

D = 2048
FF = 8192
HEADS = 16
HEAD = 128
TREE = 704
NSEG = 13
MOSTSEG = 176
TREES = 16
TOKENS = 11264


def draw_parents(key, part):
    index = jnp.arange(NSEG, dtype=jnp.int32)
    upper = jnp.maximum(index, 1)
    picked = jax.random.randint(key, (TREES, NSEG), 0, upper[None, :], dtype=jnp.int32)
    picked = jnp.where(index[None, :] == NSEG - 1, NSEG - 2, picked)
    return jnp.where(index[None, :] == 0, 0, picked).astype(jnp.int32)


def with_spikes(array, own_key, source, target, parts, factor):
    def block_of(axis_at):
        return (jnp.arange(array.shape[axis_at]) // (array.shape[axis_at] // parts)).reshape((-1,) + (1,) * (array.ndim - 1 - axis_at))

    one_side = jax.random.permutation(own_key, parts)[block_of(target)]
    other_side = (block_of(target) + parts // 2) % parts
    return jnp.where((block_of(source) == one_side) | (block_of(source) == other_side), factor * array, array)


def steps_of(own_key, shape, cuts, low, largest):
    level = 1.0
    for axis_at, shards_of in cuts:
        steps = jax.random.uniform(jax.random.fold_in(jax.random.fold_in(own_key, 6), axis_at), (shards_of,), jnp.float32, low / len(cuts), largest / len(cuts))
        level = level * jnp.repeat(jnp.exp(steps), shape[axis_at] // shards_of).reshape((-1,) + (1,) * (len(shape) - 1 - axis_at))
    return level


def profile(count, total, most, lean):
    loads = [(1 << 20) // math.isqrt(standing ** lean) + 1 for standing in range(2, count + 1)]
    spare, given = total - most - (count - 1), [1] * (count - 1)
    while spare > 0:
        candidates = [i for i in range(count - 1) if given[i] < most]
        mass, budget = sum([loads[i] for i in candidates]), spare
        for i in candidates:
            addition = min(most - given[i], max(1, budget * loads[i] // mass), spare)
            given[i] = given[i] + addition
            spare = spare - addition
    return np.array([most] + given)


def uneven_parts(own_key, number_of, total, limit, lean):
    if number_of == 2:
        one = jax.random.randint(own_key, (), max(1, total - limit), min(limit, total - 1) + 1)
        return jnp.stack([one, total - one])
    sizes = jnp.asarray(profile(number_of, total, limit, lean), jnp.int32)
    pairs = (number_of - 1) // 2
    donor, sink = sizes[1:1 + 2 * pairs:2], sizes[2:2 + 2 * pairs:2]
    slack = jnp.minimum(donor - 1, limit - sink)
    moved = jax.random.randint(jax.random.fold_in(own_key, 1), (pairs,), 0, 1 << 20) % (slack + 1)
    sizes = sizes.at[1:1 + 2 * pairs:2].set(donor - moved).at[2:2 + 2 * pairs:2].set(sink + moved)
    return sizes[jax.random.permutation(jax.random.fold_in(own_key, 2), number_of)]


def bell_draw(own_key, extent, width, limit, pieces=(), kind=jnp.bfloat16):
    values = width * jax.random.normal(own_key, extent, jnp.float32)
    if pieces:
        values = values * steps_of(own_key, extent, pieces, -0.22, 0.18)
    return jnp.clip(values, -limit, limit).astype(kind)


def heavy_noise(stream_key, shape, scale, bound, pieces, heavy, kind=jnp.bfloat16):
    result = scale * jax.random.normal(stream_key, shape, jnp.float32)
    if pieces:
        result = result * steps_of(stream_key, shape, pieces, -0.22, 0.18)
    return jnp.clip(with_spikes(result, jax.random.fold_in(stream_key, 3), *heavy), -bound, bound).astype(kind)


def setup_inputs(seed: int = 0) -> dict:
    arg_keys = jax.random.split(jax.random.key(seed), 20)
    return {
        "tokens": heavy_noise(arg_keys[0], (TOKENS, D), 1.0, 6.0, ((0, 32),), (0, 1, 32, 2.75), jnp.float32),
        "cotangent": heavy_noise(arg_keys[1], (TOKENS, D), 1.0, 6.0, ((0, 32),), (0, 1, 32, 2.75), jnp.float32),
        "lengths": jax.vmap(lambda own: uneven_parts(own, NSEG, TREE, MOSTSEG, 2))(jax.random.split(arg_keys[2], TREES)).reshape((TREES, NSEG)).astype(jnp.int32),
        "parents": draw_parents(jax.random.fold_in(arg_keys[19], 71), 0),
        "query_proj": bell_draw(arg_keys[4], (D, D), D ** -0.5, 0.125, ((0, 16), (1, 2)), jnp.float32),
        "key_proj": bell_draw(arg_keys[5], (D, D), D ** -0.5, 0.125, ((0, 16), (1, 2)), jnp.float32),
        "value_proj": bell_draw(arg_keys[6], (D, D), D ** -0.5, 0.125, ((0, 16), (1, 2)), jnp.float32),
        "out_proj": bell_draw(arg_keys[7], (D, D), (D // 8) ** -0.5, 0.375, ((0, 2), (1, 16)), jnp.float32),
        "up_proj": bell_draw(arg_keys[8], (D, FF), D ** -0.5, 0.125, ((0, 16), (1, 2)), jnp.float32),
        "down_proj": bell_draw(arg_keys[9], (FF, D), FF ** -0.5, 0.0625, ((0, 2), (1, 16)), jnp.float32),
        "first_gain": jnp.clip(1.0 + 0.1 * jax.random.normal(arg_keys[10], (D,), jnp.float32), 0.5, 1.5),
        "first_shift": bell_draw(arg_keys[11], (D,), 0.5, 3.0, ((0, 32),), jnp.float32),
        "query_bias": bell_draw(arg_keys[12], (D,), 0.5, 3.0, ((0, 32),), jnp.float32),
        "value_bias": bell_draw(arg_keys[13], (D,), 0.5, 3.0, ((0, 32),), jnp.float32),
        "out_bias": bell_draw(arg_keys[14], (D,), 0.5, 3.0, ((0, 32),), jnp.float32),
        "second_gain": jnp.clip(1.0 + 0.1 * jax.random.normal(arg_keys[15], (D,), jnp.float32), 0.5, 1.5),
        "second_shift": bell_draw(arg_keys[16], (D,), 0.5, 3.0, ((0, 32),), jnp.float32),
        "up_bias": bell_draw(arg_keys[17], (FF,), 0.5, 3.0, ((0, 32),), jnp.float32),
        "down_bias": bell_draw(arg_keys[18], (D,), 0.5, 3.0, ((0, 32),), jnp.float32),
    }


@jax.custom_vjp
def low(v):
    return lax.optimization_barrier(v.astype(jnp.bfloat16)).astype(jnp.float32)

@jax.custom_vjp
def low_back(v):
    return v

def low_keep(v):
    return (low(v), None)

def low_pass(kept, grad):
    return (grad,)

def back_keep(v):
    return (v, None)

def back_low(kept, grad):
    return (low(grad),)
low.defvjp(low_keep, low_pass)
low_back.defvjp(back_keep, back_low)
EPSILON = 1e-05
HIGHEST = lax.Precision.HIGHEST

def layer_norm(values, gain, shift):
    row_mean = lax.optimization_barrier(jnp.mean(values, axis=-1, keepdims=True))
    centred = values - row_mean
    spread = lax.optimization_barrier(jnp.mean(centred * centred, axis=-1, keepdims=True))
    return centred * lax.rsqrt(spread + EPSILON) * gain + shift

def tree_mask(seg_lengths, seg_parents):
    count = seg_lengths.shape[0]
    index = jnp.arange(count, dtype=jnp.int32)
    places = jnp.arange(TREE, dtype=jnp.int32)
    ends = jnp.cumsum(seg_lengths).astype(jnp.int32)
    segment = lax.optimization_barrier(jnp.sum((places[:, None] >= ends[None, :]).astype(jnp.int32), axis=1))
    link = ((seg_parents[:, None] == index[None, :]) & (index[:, None] > 0)).astype(jnp.float32)
    identity = jnp.eye(count, dtype=jnp.float32)
    ancestry = identity
    for step in range(count):
        ancestry = jnp.maximum(identity, jnp.dot(link, ancestry, precision=HIGHEST))
    onehot = (segment[:, None] == index[None, :]).astype(jnp.float32)
    reach = jnp.dot(jnp.dot(onehot, ancestry, precision=HIGHEST), onehot.T, precision=HIGHEST) > 0.5
    return reach & (places[None, :] <= places[:, None])

def attend(block):
    queries, key_rows, value_rows, seg_lengths, seg_parents = block
    allowed = tree_mask(seg_lengths, seg_parents)
    scores = jnp.einsum('qhd,khd->hqk', queries, key_rows, precision=HIGHEST) * HEAD ** (-0.5)
    scores = low_back(scores)
    scores = jnp.where(allowed[None], scores, -jnp.inf)
    top = lax.optimization_barrier(jnp.max(scores, axis=-1, keepdims=True))
    expos = jnp.exp(scores - top)
    probs = expos / lax.optimization_barrier(jnp.sum(expos, axis=-1, keepdims=True))
    probs = low(probs)
    return jnp.einsum('hqk,khd->qhd', probs, value_rows, precision=HIGHEST)

def reference(tokens, cotangent, lengths, parents, query_proj, key_proj, value_proj, out_proj, up_proj, down_proj, first_gain, first_shift, query_bias, value_bias, out_bias, second_gain, second_shift, up_bias, down_bias):

    def forward(inputs, w_query, w_key, w_value, w_out, w_up, w_down, gain_one, shift_one, bias_query, bias_value, bias_out, gain_two, shift_two, bias_up, bias_down):
        first_rows = low(layer_norm(inputs, gain_one, shift_one))
        queries = low_back(low(jnp.dot(first_rows, low(w_query), precision=HIGHEST) + bias_query))
        key_rows = low_back(low(jnp.dot(first_rows, low(w_key), precision=HIGHEST)))
        value_rows = low_back(low(jnp.dot(first_rows, low(w_value), precision=HIGHEST) + bias_value))
        shape4 = (TREES, TREE, HEADS, HEAD)
        mixed = lax.map(jax.checkpoint(attend), (queries.reshape(shape4), key_rows.reshape(shape4), value_rows.reshape(shape4), lengths, parents))
        mixed_rows = low_back(low(mixed.reshape(TOKENS, D)))
        middle = inputs + low_back(jnp.dot(mixed_rows, low(w_out), precision=HIGHEST) + bias_out)
        second_rows = low(layer_norm(middle, gain_two, shift_two))
        pre_act = low_back(jnp.dot(second_rows, low(w_up), precision=HIGHEST) + bias_up)
        act_rows = low(jax.nn.gelu(pre_act, approximate=False))
        return middle + low_back(jnp.dot(act_rows, low(w_down), precision=HIGHEST) + bias_down)
    output, pull = jax.vjp(forward, tokens, query_proj, key_proj, value_proj, out_proj, up_proj, down_proj, first_gain, first_shift, query_bias, value_bias, out_bias, second_gain, second_shift, up_bias, down_bias)
    grads = pull(cotangent)
    return (output, grads[0], grads[1], grads[2], grads[3], grads[4], grads[5], grads[6], grads[7], grads[8], grads[9], grads[10], grads[11], grads[12], grads[13], grads[14], grads[15])
```

```python
import functools

import jax
import jax.numpy as jnp
import numpy as np
from jax import lax
from jax.experimental import pallas as pl
from jax.experimental.pallas import tpu as pltpu
from jax.sharding import PartitionSpec as P

HEAD = 128
EPSILON = 1e-05
MASKED = -1e30
SCALE = HEAD ** (-0.5)
F32 = jnp.float32
BF16 = jnp.bfloat16
CONTRACT_ROWS = (((0,), (0,)), ((), ()))
CONTRACT_COLS = (((1,), (1,)), ((), ()))


def dot(a, b):
    return jnp.dot(a, b, preferred_element_type=F32)


def dot_cols(a, b):
    return lax.dot_general(a, b, CONTRACT_COLS, preferred_element_type=F32)


def dot_rows(a, b):
    return lax.dot_general(a, b, CONTRACT_ROWS, preferred_element_type=F32)


def row_slice(values, start, size, axis=0):
    return lax.dynamic_slice_in_dim(values, start, size, axis=axis)


def gate(value, *waits):
    return lax.optimization_barrier((value,) + waits)[0]


def query_blocks(total):
    blocks = []
    start = 0
    while start < total:
        size = min(256, total - start)
        blocks.append((start, size))
        start += size
    return blocks


def attend_kernel(qkv_ref, bias_ref, mixed_ref, lse_ref):
    total = qkv_ref.shape[0]
    for start, size in query_blocks(total):
        stop = start + size
        query = qkv_ref[start:stop, :HEAD]
        key = qkv_ref[:stop, HEAD : 2 * HEAD]
        value = qkv_ref[:stop, 2 * HEAD :]
        scores = dot_cols(query, key) * SCALE + bias_ref[0, start:stop, :stop]
        top = jnp.max(scores, axis=-1, keepdims=True)
        expos = jnp.exp(scores - top)
        total_exp = jnp.sum(expos, axis=-1, keepdims=True)
        probs = (expos * (1.0 / total_exp)).astype(BF16)
        mixed_ref[start:stop, :] = dot(probs, value).astype(BF16)
        lse_ref[start:stop, :] = jnp.broadcast_to(top + jnp.log(total_exp), (size, HEAD))


def attend_back_kernel(qkv_ref, bias_ref, lse_ref, grad_ref, out_ref, key_acc, value_acc):
    total = qkv_ref.shape[0]
    for start, size in reversed(query_blocks(total)):
        stop = start + size
        query = qkv_ref[start:stop, :HEAD]
        key = qkv_ref[:stop, HEAD : 2 * HEAD]
        value = qkv_ref[:stop, 2 * HEAD :]
        grad = grad_ref[start:stop, :]
        scores = dot_cols(query, key) * SCALE + bias_ref[0, start:stop, :stop]
        probs = jnp.exp(scores - lse_ref[start:stop, :1])
        value_part = dot_rows(probs.astype(BF16), grad)
        prob_grad = dot_cols(grad, value)
        inner = jnp.sum(probs * prob_grad, axis=-1, keepdims=True)
        score_grad = (probs * (prob_grad - inner)).astype(BF16)
        out_ref[start:stop, :HEAD] = (dot(score_grad, key) * SCALE).astype(BF16)
        key_part = dot_rows(score_grad, query)
        if stop == total:
            key_acc[...] = key_part
            value_acc[...] = value_part
        else:
            key_acc[:stop, :] += key_part
            value_acc[:stop, :] += value_part
    out_ref[:, HEAD : 2 * HEAD] = (key_acc[...] * SCALE).astype(BF16)
    out_ref[:, 2 * HEAD :] = value_acc[...].astype(BF16)


def attend(qkv, bias):
    trees, tree, _ = bias.shape
    heads = qkv.shape[1] // (3 * HEAD)
    return pl.pallas_call(
        attend_kernel,
        grid=(trees, heads),
        in_specs=[
            pl.BlockSpec((tree, 3 * HEAD), lambda t, h: (t, h)),
            pl.BlockSpec((1, tree, tree), lambda t, h: (t, 0, 0)),
        ],
        out_specs=[
            pl.BlockSpec((tree, HEAD), lambda t, h: (t, h)),
            pl.BlockSpec((tree, HEAD), lambda t, h: (t, h)),
        ],
        out_shape=[
            jax.ShapeDtypeStruct((trees * tree, heads * HEAD), BF16),
            jax.ShapeDtypeStruct((trees * tree, heads * HEAD), F32),
        ],
        name="attend",
    )(qkv, bias)


def attend_back(qkv, bias, lse, grad):
    trees, tree, _ = bias.shape
    heads = qkv.shape[1] // (3 * HEAD)
    return pl.pallas_call(
        attend_back_kernel,
        grid=(trees, heads),
        in_specs=[
            pl.BlockSpec((tree, 3 * HEAD), lambda t, h: (t, h)),
            pl.BlockSpec((1, tree, tree), lambda t, h: (t, 0, 0)),
            pl.BlockSpec((tree, HEAD), lambda t, h: (t, h)),
            pl.BlockSpec((tree, HEAD), lambda t, h: (t, h)),
        ],
        out_specs=pl.BlockSpec((tree, 3 * HEAD), lambda t, h: (t, h)),
        out_shape=jax.ShapeDtypeStruct(qkv.shape, BF16),
        scratch_shapes=[pltpu.VMEM((tree, HEAD), F32), pltpu.VMEM((tree, HEAD), F32)],
        name="attend_back",
    )(qkv, bias, lse, grad)


def norm_parts(values):
    mean = jnp.mean(values, axis=-1, keepdims=True)
    centred = values - mean
    spread = jnp.mean(centred * centred, axis=-1, keepdims=True)
    inverse = lax.rsqrt(spread + EPSILON)
    return centred * inverse, inverse


def norm_back(grad, gain, normal, inverse):
    scaled = grad * gain
    mean_one = jnp.mean(scaled, axis=-1, keepdims=True)
    mean_two = jnp.mean(scaled * normal, axis=-1, keepdims=True)
    back = (scaled - mean_one - normal * mean_two) * inverse
    return back, jnp.sum(grad * normal, axis=0), jnp.sum(grad, axis=0)


def gelu_pair(values):
    half = 0.5 * (1.0 + lax.erf(values * np.float32(np.sqrt(0.5))))
    density = jnp.exp(-0.5 * values * values) * np.float32(1.0 / np.sqrt(2.0 * np.pi))
    return values * half, half + values * density


def column_sums(values):
    return jnp.sum(values.astype(F32), axis=0)


def tree_bias(seg_lengths, seg_parents, total):
    count = seg_lengths.shape[0]
    index = jnp.arange(count, dtype=jnp.int32)
    places = jnp.arange(total, dtype=jnp.int32)
    ends = jnp.sum(
        jnp.where(index[None, :] <= index[:, None], seg_lengths[None, :], 0), axis=1
    )
    segment = jnp.sum((places[:, None] >= ends[None, :]).astype(jnp.int32), axis=1)
    link = ((seg_parents[:, None] == index[None, :]) & (index[:, None] > 0)) | (
        index[:, None] == index[None, :]
    )
    paths = link.astype(F32)
    reached = 1
    while reached < count - 1:
        paths = jnp.minimum(dot(paths, paths), 1.0)
        reached *= 2
    onehot = (segment[:, None] == index[None, :]).astype(F32)
    reach = dot_cols(dot(onehot, paths), onehot) > 0.5
    return jnp.where(reach & (places[None, :] <= places[:, None]), 0.0, MASKED)


def local(
    chips,
    tokens,
    cotangent,
    lengths,
    parents,
    query_proj,
    key_proj,
    value_proj,
    out_proj,
    up_proj,
    down_proj,
    first_gain,
    first_shift,
    query_bias,
    value_bias,
    out_bias,
    second_gain,
    second_shift,
    up_bias,
    down_bias,
):
    place = lax.axis_index("dp")
    chip = place // 2
    core = place % 2
    part = lax.axis_index("tensor")
    ring = list(range(0, chips, 2)) + list(range(chips - 1, 0, -2))
    half = chips // 2
    spots = np.argsort(np.array(ring))
    table = np.array(
        [[ring[(spots[c] + k) % chips] for k in range(chips)] for c in range(chips)], np.int32
    )
    around = jnp.asarray(table)[chip]

    def chip_perm(pairs):
        return [(2 * a + c, 2 * b + c) for a, b in pairs for c in range(2)]

    ahead_pairs = chip_perm([(ring[i], ring[(i + 1) % chips]) for i in range(chips)])
    behind_pairs = [(b, a) for a, b in ahead_pairs]
    core_pairs = [(i, i ^ 1) for i in range(2 * chips)]
    ahead = lambda v: lax.ppermute(v, "dp", ahead_pairs)
    behind = lambda v: lax.ppermute(v, "dp", behind_pairs)
    swap_core = lambda v: lax.ppermute(v, "dp", core_pairs)
    swap_part = lambda v: lax.ppermute(v, "tensor", [(0, 1), (1, 0)])

    def ordered(first, own, other, axis):
        return jnp.where(
            first,
            jnp.concatenate([own, other], axis=axis),
            jnp.concatenate([other, own], axis=axis),
        )

    def ring_gather(chunk):
        rows = chunk.shape[0]
        fore, back = chunk, chunk
        pieces = [(0, 0, chunk)]
        for step in range(1, half):
            fore = ahead(fore)
            back = behind(back)
            pieces.append((-step, 0, fore))
            pieces.append((step, 0, back))
        pieces.append((half, 0, ahead(fore[: rows // 2])))
        pieces.append((half, rows // 2, behind(back[rows // 2 :])))
        return pieces

    def assemble(pieces, full, rows, column, crop=None):
        for offset, shift, piece in pieces:
            if crop is not None:
                piece = piece[:, crop]
            full = lax.dynamic_update_slice(
                full, piece, (around[offset % chips] * rows + shift, column)
            )
        return full

    def ring_sum(contribution, waits=()):
        fore = back = None
        for step in range(half, 0, -1):
            add_f, add_b = contribution(step), contribution(-step)
            if step == half:
                rows = add_f.shape[0]
                send_f = add_f[: rows // 2].astype(BF16)
                send_b = add_f[rows // 2 :].astype(BF16)
            elif step == half - 1:
                pad = ((0, rows // 2), (0, 0))
                dap = ((rows // 2, 0), (0, 0))
                send_f = (add_f + jnp.pad(fore, pad).astype(F32)).astype(BF16)
                send_b = (add_b + jnp.pad(back, dap).astype(F32)).astype(BF16)
            else:
                send_f = (add_f + fore.astype(F32)).astype(BF16)
                send_b = (add_b + back.astype(F32)).astype(BF16)
            fore = ahead(send_f)
            back = behind(send_b)
        return contribution(0) + fore.astype(F32) + back.astype(F32)

    def gather_vectors(own):
        held = own[None]
        held = ordered(part == 0, held, swap_part(held), 0)
        bits = [(core, 1)]
        bit = 1
        while bit < chips:
            bits.append(((chip // bit) % 2, 2 * bit))
            bit *= 2
        for side, flip in bits:
            other = lax.ppermute(held, "dp", [(i, i ^ flip) for i in range(2 * chips)])
            held = ordered(side == 0, held, other, 0)
        return held

    def scatter_vectors(held):
        bits = []
        bit = chips // 2
        while bit >= 1:
            bits.append(((chip // bit) % 2, 2 * bit))
            bit //= 2
        bits.append((core, 1))
        for side, flip in bits:
            rows = held.shape[0] // 2
            other = lax.ppermute(
                row_slice(held, (1 - side) * rows, rows),
                "dp",
                [(i, i ^ flip) for i in range(2 * chips)],
            )
            held = row_slice(held, side * rows, rows) + other
        other = swap_part(row_slice(held, 1 - part, 1))
        return (row_slice(held, part, 1) + other)[0]

    owned, width = tokens.shape
    tree = 2 * owned
    inner = query_proj.shape[1] // 2
    hidden = up_proj.shape[1] // 2
    rows = 2 * query_proj.shape[0]
    heads = inner // HEAD

    def gather_rows(own):
        peer = swap_part(own)
        near = swap_core(own)
        far = swap_core(peer)
        full = jnp.zeros((2 * tree, own.shape[1]), own.dtype)
        for value, start in (
            (own, part * owned),
            (near, tree + part * owned),
            (peer, (1 - part) * owned),
            (far, tree + (1 - part) * owned),
        ):
            full = lax.dynamic_update_slice_in_dim(full, value, start, axis=0)
        return full

    def sum_rows(product, values):
        other = swap_core(product(values[tree:]).astype(BF16))
        held = product(values[:tree]) + other.astype(F32)
        peer = swap_part(row_slice(held, (1 - part) * owned, owned).astype(BF16))
        return row_slice(held, part * owned, owned) + peer.astype(F32)

    def swapped(shard, cut):
        own = row_slice(shard, core * cut, cut, axis=shard.ndim - 1)
        other = row_slice(shard, (1 - core) * cut, cut, axis=shard.ndim - 1)
        return ordered(core == 0, own, swap_core(other), 0)

    def by_head(values):
        return values.reshape(values.shape[0], -1, HEAD)

    stacked = jnp.stack(
        [by_head(w.astype(BF16)) for w in (query_proj, key_proj, value_proj)], axis=2
    ).reshape(query_proj.shape[0], -1)
    qkv_chunk = swapped(stacked, 3 * inner)
    out_chunk = swapped(out_proj.astype(BF16).T, inner)
    up_chunk = swapped(up_proj.astype(BF16), hidden)
    down_chunk = swapped(down_proj.astype(BF16).T, hidden)

    qkv_pieces = ring_gather(qkv_chunk)
    out_pieces = ring_gather(gate(out_chunk, qkv_pieces[1][2], qkv_pieces[2][2]))
    up_pieces = ring_gather(gate(up_chunk, qkv_pieces[-3][2], qkv_pieces[-4][2]))
    down_pieces = ring_gather(gate(down_chunk, up_pieces[-3][2], up_pieces[-4][2]))
    w_qkv = assemble(qkv_pieces, jnp.zeros((width, 3 * inner), BF16), rows, 0)
    w_out = assemble(out_pieces, jnp.zeros((width, inner), BF16), rows, 0)
    w_up = assemble(up_pieces, jnp.zeros((width, hidden), BF16), rows, 0)
    w_down = assemble(down_pieces, jnp.zeros((width, hidden), BF16), rows, 0)

    small = (
        first_gain,
        first_shift,
        query_bias,
        value_bias,
        out_bias,
        second_gain,
        second_shift,
        up_bias,
        down_bias,
    )
    cuts = np.cumsum([0] + [v.shape[0] for v in small])
    every = gather_vectors(jnp.concatenate(small))
    (gain_one, shift_one, query_full, value_full, out_full, gain_two, shift_two, up_full, down_full) = (
        every[:, cuts[i] : cuts[i + 1]].reshape(-1) for i in range(9)
    )
    quarter = 2 * part + core
    query_local = row_slice(query_full, quarter * inner, inner).reshape(heads, HEAD)
    value_local = row_slice(value_full, quarter * inner, inner).reshape(heads, HEAD)
    qkv_local = jnp.stack([query_local, jnp.zeros_like(query_local), value_local], axis=1).reshape(-1)
    up_local = row_slice(up_full, quarter * hidden, hidden)

    meta = jnp.concatenate([lengths, parents], axis=0)
    other_meta = swap_core(meta)
    bias = jnp.stack(
        [tree_bias(meta[0], meta[1], tree), tree_bias(other_meta[0], other_meta[1], tree)]
    )

    normal_one, inverse_one = norm_parts(tokens)
    attn_in = gather_rows((normal_one * gain_one + shift_one).astype(BF16))
    down_cot = cotangent.astype(BF16)
    down_all = gather_rows(down_cot)
    qkv = (dot(attn_in, w_qkv) + qkv_local).astype(BF16)
    mixed, lse = attend(qkv, bias)
    middle = tokens + sum_rows(lambda v: dot_cols(v, w_out), mixed) + out_full
    normal_two, inverse_two = norm_parts(middle)
    ffwd_in = gather_rows((normal_two * gain_two + shift_two).astype(BF16))
    activ, slope = gelu_pair(dot(ffwd_in, w_up) + up_local)
    act_rows = activ.astype(BF16)
    layer_output = middle + sum_rows(lambda v: dot_cols(v, w_down), act_rows) + down_full

    def chunk_of(values, offset):
        return row_slice(values, around[offset % chips] * rows, rows, axis=1)

    down_sum = ring_sum(lambda k: dot_rows(chunk_of(down_all, k), act_rows))
    pre_rows = (dot(down_all, w_down) * slope).astype(BF16)
    up_bias_grad = column_sums(pre_rows)
    up_sum = ring_sum(lambda k: dot_rows(chunk_of(ffwd_in, k), pre_rows))
    second_in = sum_rows(lambda v: dot_cols(v, w_up), pre_rows)
    middle_part, gain_two_grad, shift_two_grad = norm_back(
        second_in, gain_two, normal_two, inverse_two
    )
    middle_grad = cotangent + middle_part

    attn_cot = middle_grad.astype(BF16)
    attn_all = gather_rows(attn_cot)
    mixed_grad = dot(attn_all, w_out).astype(BF16)
    qkv_grad = attend_back(qkv, bias, lse, mixed_grad)
    out_sum = ring_sum(lambda k: dot_rows(chunk_of(attn_all, k), mixed))
    qkv_sum = ring_sum(lambda k: dot_rows(chunk_of(attn_in, k), qkv_grad))
    first_in = sum_rows(lambda v: dot_cols(v, w_qkv), qkv_grad)
    tokens_part, gain_one_grad, shift_one_grad = norm_back(
        first_in, gain_one, normal_one, inverse_one
    )
    tokens_grad = middle_grad + tokens_part

    bias_sums = column_sums(qkv_grad).reshape(heads, 3, HEAD)
    spread = lambda values, size: lax.dynamic_update_slice_in_dim(
        jnp.zeros((size,), F32), values, quarter * values.shape[0], 0
    )
    sums = (
        gain_one_grad,
        shift_one_grad,
        spread(bias_sums[:, 0].reshape(-1), width),
        spread(bias_sums[:, 2].reshape(-1), width),
        column_sums(attn_cot),
        gain_two_grad,
        shift_two_grad,
        spread(up_bias_grad, up_full.shape[0]),
        column_sums(down_cot),
    )
    vector_sum = scatter_vectors(
        jnp.concatenate([v.reshape(4 * chips, -1) for v in sums], axis=1)
    )
    vector_grads = tuple(vector_sum[cuts[i] : cuts[i + 1]] for i in range(9))

    def returned(total):
        cut = rows // 2
        own = row_slice(total, core * cut, cut)
        other = swap_core(row_slice(total, (1 - core) * cut, cut))
        return ordered(core == 0, own, other, 1)

    qkv_back = returned(qkv_sum).reshape(rows // 2, 2 * heads, 3, HEAD)
    return (
        layer_output,
        tokens_grad,
        qkv_back[:, :, 0].reshape(rows // 2, -1),
        qkv_back[:, :, 1].reshape(rows // 2, -1),
        qkv_back[:, :, 2].reshape(rows // 2, -1),
        returned(out_sum).T,
        returned(up_sum),
        returned(down_sum).T,
    ) + vector_grads


def solution(mesh):
    tokens_place = P(("dp", "tensor"), None)
    trees_place = P("dp", None)
    rows_place = P("dp", "tensor")
    columns_place = P("tensor", "dp")
    vector_place = P(("dp", "tensor"))
    weights = (rows_place, rows_place, rows_place, columns_place, rows_place, columns_place)
    return jax.shard_map(
        functools.partial(local, mesh.shape["dp"] // 2),
        mesh=mesh,
        in_specs=(tokens_place, tokens_place, trees_place, trees_place)
        + weights
        + (vector_place,) * 9,
        out_specs=(tokens_place, tokens_place) + weights + (vector_place,) * 9,
        check_vma=False,
    )
```
